32 devices in a mesh: group: 2 (over y), sta: 4 (over z), win: 2 (over x), freq: 2 (over core).
Axes of the slice: x: 2, y: 2, z: 4, core: 2. Of those that a mesh axis runs over, the one named last changes fastest.
Arguments:
- records: float32 [1024, 4, 3600], P(('group', 'sta'), 'win', 'freq'), parts along dimension 0, may hold values from -6 to 6
- valid_counts: int32 [8], P(('group', 'sta')), parts along dimension 0, may hold values from 64 to 128, as said below
- pair_blocks: int32 [8, 2], P('group'), parts along dimension 0, may hold values from 0 to 3, as said below
Outputs:
- pair_spectra: bfloat16 [8, 2, 256, 2, 128, 128], P(('group', 'sta'), 'freq', 'win'), parts along dimension 0
The draws below stay inside these ranges and needn't reach their ends.
There are 2 independent parts, one for each index of `group`. The reference program is written for one: setup_inputs(seed, part) draws one part's arguments, and reference() takes and returns one part's arrays. A program takes and returns all parts, laid end to end along the dimension named above; each array names one. Nothing has to cross between parts.
Inputs may be any that keep to these rules, and one draw needn't show every extreme that they name: The stations of block i at positions below valid_counts[i] are live, the others are masked out. `pair_blocks`: slot k belongs to index k // 1 of sta and names two station blocks.
All inputs are finite; a program needn't handle non-finite values.
Results may differ from the reference program's by a relative error of at most 0.001.
Values may be sent and summed in bfloat16 or wider, within the bound.
A program may use at most 64 MiB of HBM per device.

```python
import math
import jax
import jax.numpy as jnp
from jax import lax

BLOCK = 128
SAMPLES = 3600
BINS = 512
HALF_WIDTH = 10
PAIR_DEV = 1
NBLOCKS = 4
STATIONS = 512
WINDOWS = 4
NPAIR = 4
BANDS = 2
BAND = 256


def draw_valid_counts(key, part):
    counts = jax.random.randint(key, (NBLOCKS,), BLOCK // 2, BLOCK + 1)
    full_block = jax.random.randint(jax.random.fold_in(key, 1), (), 0, NBLOCKS)
    counts = counts.at[full_block].set(BLOCK)
    low_block = (full_block + 1 + jax.random.randint(jax.random.fold_in(key, 2), (), 0, NBLOCKS - 1)) % NBLOCKS
    return counts.at[low_block].set(BLOCK // 2).astype(jnp.int32)


def draw_pair_blocks(key, part):
    slot_ids = jnp.arange(NPAIR, dtype=jnp.int32)
    owners = slot_ids // PAIR_DEV
    offset_base = jax.random.randint(jax.random.fold_in(key, 11), (), 0, NBLOCKS - 1)
    reach = 1 + (slot_ids + offset_base) % (NBLOCKS - 1)
    second = (owners + reach) % NBLOCKS
    firsts = jnp.tile(jax.random.permutation(jax.random.fold_in(key, 12), NBLOCKS).astype(jnp.int32), PAIR_DEV)
    return jnp.stack((firsts, second), axis=1).astype(jnp.int32)


def shard_levels(own_key, dims, cuts, least, high):
    level = 1.0
    for axis_at, parts in cuts:
        steps = jax.random.uniform(jax.random.fold_in(jax.random.fold_in(own_key, 6), axis_at), (parts,), jnp.float32, least / len(cuts), high / len(cuts))
        level = level * jnp.repeat(jnp.exp(steps), dims[axis_at] // parts).reshape((-1,) + (1,) * (len(dims) - 1 - axis_at))
    return level


def normal_values(stream_key, extent, deviation, limit, shards=(), kind=jnp.bfloat16):
    gain = shard_levels(stream_key, extent, shards, -0.22, 0.18) if shards else 1.0
    values = jax.random.normal(stream_key, extent, jnp.float32) * deviation * gain
    return jnp.minimum(jnp.maximum(values, -limit), limit).astype(kind)


def setup_inputs(seed: int = 0, part: int = 0) -> dict:
    arg_keys = jax.random.split(jax.random.key(seed), 4)
    own_keys = jax.random.split(jax.random.fold_in(arg_keys[3], part), 4)
    return {
        "records": normal_values(own_keys[0], (STATIONS, WINDOWS, SAMPLES), 1.0, 6.0, ((0, 4), (1, 2), (2, 2)), jnp.float32),
        "valid_counts": draw_valid_counts(jax.random.fold_in(jax.random.fold_in(arg_keys[3], part), 71), part),
        "pair_blocks": draw_pair_blocks(jax.random.fold_in(jax.random.fold_in(arg_keys[3], part), 71), part),
    }


TWO_PI = 2.0 * math.pi
AMP_FLOOR = 0.1
PRECISE = lax.Precision.HIGHEST

def taper_of(sample_index, length_all):
    edge_len = length_all // 20
    position = jnp.minimum(sample_index, length_all - 1 - sample_index)
    ramped = 0.5 * (1.0 - jnp.cos(math.pi * (position.astype(jnp.float32) + 0.5) / edge_len))
    return jnp.where(position < edge_len, ramped, 1.0)

def dft_tables(bin_start, amount, sample_start, sample_count, length_all):
    bin_index = bin_start + 1 + lax.broadcasted_iota(jnp.int32, (amount, sample_count), 0)
    sample_index = sample_start + lax.broadcasted_iota(jnp.int32, (amount, sample_count), 1)
    angles = (bin_index * sample_index % length_all).astype(jnp.float32) * (TWO_PI / length_all)
    weight = taper_of(sample_index, length_all) / math.sqrt(length_all)
    return (jnp.cos(angles) * weight, -jnp.sin(angles) * weight)

def whiten_block(block_records, live_count):
    cos_table, sin_table = dft_tables(0, BINS, 0, SAMPLES, SAMPLES)
    real_part = jnp.einsum('kn,swn->kws', cos_table, block_records, precision=PRECISE)
    imag_part = jnp.einsum('kn,swn->kws', sin_table, block_records, precision=PRECISE)
    live_mask = (jnp.arange(BLOCK, dtype=jnp.int32) < live_count).astype(jnp.float32)
    spectrum = jnp.stack((real_part, imag_part), 2) * live_mask
    magnitude = jnp.sqrt(spectrum[:, :, 0] * spectrum[:, :, 0] + spectrum[:, :, 1] * spectrum[:, :, 1])
    padded = jnp.pad(magnitude, ((HALF_WIDTH, HALF_WIDTH), (0, 0), (0, 0)))
    summed = padded[0:BINS]
    for lag_step in range(1, 2 * HALF_WIDTH + 1):
        summed = summed + padded[lag_step:lag_step + BINS]
    global_bin = jnp.arange(BINS, dtype=jnp.int32)
    counted = (jnp.minimum(global_bin + HALF_WIDTH, BINS - 1) - jnp.maximum(global_bin - HALF_WIDTH, 0) + 1).astype(jnp.float32)
    smooth = summed / counted[:, None, None]
    return spectrum / jnp.maximum(smooth, AMP_FLOOR)[:, :, None, :]

def cross_pair(left_block, right_block):
    left_real = left_block[:, :, 0]
    left_imag = left_block[:, :, 1]
    stacked = jnp.stack((jnp.stack((left_real, left_imag), 2), jnp.stack((left_imag, -left_real), 2)), 1)
    factor = 1.0 / math.sqrt(left_block.shape[1])
    return jnp.einsum('fpwqa,fwqb->fpab', stacked, right_block, precision=PRECISE) * factor

def reference(records, valid_counts, pair_blocks):
    grouped = records.reshape(NBLOCKS, BLOCK, WINDOWS, SAMPLES)

    def whiten_item(item_pair):
        return whiten_block(item_pair[0], item_pair[1])
    spectra = lax.map(whiten_item, (grouped, valid_counts))

    def one_pair(pair_row):
        left_block = spectra[pair_row[0]]
        right_block = spectra[pair_row[1]]
        return cross_pair(left_block, right_block).astype(jnp.bfloat16)
    result = lax.map(one_pair, pair_blocks)
    return result.reshape(NPAIR, BANDS, BAND, 2, BLOCK, BLOCK)
```

```python
import functools
import math

import jax
import jax.numpy as jnp
import numpy as np
from jax import lax
from jax.experimental import pallas as pl
from jax.experimental.pallas import tpu as pltpu
from jax.sharding import PartitionSpec as P

SAMPLES = 3600
BINS = 512
HALF_WIDTH = 10
AMP_FLOOR = 0.1
HALO = 16
PAD = 1920
BAND = BINS // 2
ROWS = BAND + HALO
LEVELS = 32766.0
MESH = pl.DeviceIdType.MESH


def band_bins(band):
    own = np.arange(BAND) + band * BAND
    halo = np.arange(HALO) + (BAND if band == 0 else BAND - HALO)
    return np.concatenate([own, halo])


def dft_table():
    half = SAMPLES // 2
    table = np.zeros((2, 2, 2, ROWS, PAD), jnp.bfloat16)
    for band in range(2):
        phase = (band_bins(band)[:, None] + 1) * np.arange(half)[None] % SAMPLES
        angle = phase * (2.0 * math.pi / SAMPLES)
        for part, value in enumerate((np.cos(angle), -np.sin(angle))):
            high = value.astype(jnp.bfloat16)
            table[band, part, 0, :, :half] = high
            table[band, part, 1, :, :half] = (value - high.astype(np.float64)).astype(jnp.bfloat16)
    return table


def split(value):
    high = value.astype(jnp.bfloat16)
    return high, (value - high.astype(jnp.float32)).astype(jnp.bfloat16)


def dot_nt(a, b):
    return lax.dot_general(a, b, (((1,), (1,)), ((), ())), preferred_element_type=jnp.float32)


def spectra_kernel(
    stas, wins, local_wins, x_ref, table_ref, out_ref,
    tab, xh, xl, give, got, own, codes,
    tab_sem, fs_sem, fr_sem, ws_sem, wr_sem, rs_sem, rr_sem, ls_sem, lr_sem, own_sem,
):
    sta = lax.axis_index("sta")
    win = lax.axis_index("win")
    freq = lax.axis_index("freq")
    other = 1 - freq
    cols = x_ref.shape[0]
    lanes = cols // local_wins
    sub = BAND // wins
    has_right = sta < stas - 1
    has_left = sta > 0

    def table_copy(step):
        band = other if step < 2 else freq
        return pltpu.make_async_copy(
            table_ref.at[band, step % 2], tab.at[step], tab_sem.at[step]
        )

    for step in range(4):
        table_copy(step).start()

    barrier = pltpu.get_barrier_semaphore()
    pl.semaphore_signal(barrier, inc=1, device_id={"freq": other}, device_id_type=MESH)
    for hop in range(1, wins):
        pl.semaphore_signal(
            barrier, inc=1, device_id={"win": lax.rem(win + hop, wins)}, device_id_type=MESH
        )

    @pl.when(has_right)
    def _():
        pl.semaphore_signal(barrier, inc=1, device_id={"sta": sta + 1}, device_id_type=MESH)

    @pl.when(has_left)
    def _():
        pl.semaphore_signal(barrier, inc=1, device_id={"sta": sta - 1}, device_id_type=MESH)

    high, low = split(x_ref[...])
    xh[...] = high
    xl[...] = low

    ends = jnp.where(has_right, 1, 0) + jnp.where(has_left, 1, 0)
    pl.semaphore_wait(barrier, wins + ends)

    odd = lax.broadcasted_iota(jnp.int32, (ROWS, 1), 0) % 2
    sign = jnp.where((odd == 0) & (freq == 1), -1.0, 1.0).astype(jnp.float32)

    def partial(step):
        table_copy(step).wait()
        value = dot_nt(tab[step, 0], xh[...]) + (
            dot_nt(tab[step, 0], xl[...]) + dot_nt(tab[step, 1], xh[...])
        )
        return value * sign

    def freq_copy(step):
        return pltpu.make_async_remote_copy(
            src_ref=give.at[step], dst_ref=got.at[step],
            send_sem=fs_sem.at[step], recv_sem=fr_sem.at[step],
            device_id={"freq": other}, device_id_type=MESH,
        )

    for step in range(2):
        give[step] = partial(step)
        freq_copy(step).start()
    for step in range(2):
        own[step] = partial(2 + step)
    for step in range(2):
        freq_copy(step).wait()

    real = own[0] + got[0]
    imag = own[1] + got[1]
    magnitude = jnp.sqrt(real * real + imag * imag)
    row = lax.broadcasted_iota(jnp.int32, (BAND, ROWS), 0)
    col = lax.broadcasted_iota(jnp.int32, (BAND, ROWS), 1)
    place = jnp.where(col < BAND, col, jnp.where(freq == 0, col, col - BAND - HALO))
    box = ((place - row <= HALF_WIDTH) & (row - place <= HALF_WIDTH)).astype(jnp.float32)
    box = box.astype(jnp.bfloat16)
    mag_high, mag_low = split(magnitude)
    summed = jnp.dot(box, mag_high, preferred_element_type=jnp.float32) + jnp.dot(
        box, mag_low, preferred_element_type=jnp.float32
    )
    bin_at = freq * BAND + lax.broadcasted_iota(jnp.int32, (BAND, 1), 0)
    counted = (
        jnp.minimum(bin_at + HALF_WIDTH, BINS - 1) - jnp.maximum(bin_at - HALF_WIDTH, 0) + 1
    ).astype(jnp.float32)
    inverse = 1.0 / jnp.maximum(summed / counted, AMP_FLOOR)
    real = real[:BAND] * inverse
    imag = imag[:BAND] * inverse

    for dest in range(wins):
        for w in range(local_wins):
            re = real[dest * sub:(dest + 1) * sub, w * lanes:(w + 1) * lanes]
            im = imag[dest * sub:(dest + 1) * sub, w * lanes:(w + 1) * lanes]
            peak = jnp.max(jnp.maximum(jnp.abs(re), jnp.abs(im)), axis=0, keepdims=True)
            level = jnp.ceil(jnp.log2(jnp.maximum(peak, 1e-30)) * 4.0 + 0.01)
            factor = jnp.exp2(level * -0.25) * LEVELS
            top = jnp.round(re * factor).astype(jnp.int32)
            bottom = jnp.round(im * factor).astype(jnp.int32)
            codes[dest, pl.ds(w, sub, stride=local_wins), :] = top * 65536 + (bottom & 65535)
            codes[dest, pl.ds(sub * local_wins + w, 1), :] = level.astype(jnp.int32)

    def win_copy(hop):
        to = lax.rem(win + hop, wins)
        return pltpu.make_async_remote_copy(
            src_ref=codes.at[to], dst_ref=out_ref.at[sta, win],
            send_sem=ws_sem.at[hop], recv_sem=wr_sem.at[hop],
            device_id={"win": to}, device_id_type=MESH,
        )

    for hop in range(1, wins):
        win_copy(hop).start()
    keep = pltpu.make_async_copy(codes.at[win], out_ref.at[sta, win], own_sem)
    keep.start()
    keep.wait()

    def slot(block, j):
        return out_ref.at[block, lax.rem(win - j + wins, wins)]

    def right_copy(block, t, j):
        return pltpu.make_async_remote_copy(
            src_ref=slot(block, j), dst_ref=slot(block, j),
            send_sem=rs_sem.at[t, j], recv_sem=rr_sem.at[t, j],
            device_id={"sta": sta + 1}, device_id_type=MESH,
        )

    def left_copy(block, t, j):
        return pltpu.make_async_remote_copy(
            src_ref=slot(block, j), dst_ref=slot(block, j),
            send_sem=ls_sem.at[t, j], recv_sem=lr_sem.at[t, j],
            device_id={"sta": sta - 1}, device_id_type=MESH,
        )

    for j in range(wins):
        if j > 0:
            win_copy(j).wait_recv()

        @pl.when(has_right)
        def _(j=j):
            right_copy(sta, 0, j).start()

        @pl.when(has_left)
        def _(j=j):
            left_copy(sta, 0, j).start()

    def relay(t, carry):
        for j in range(wins):
            @pl.when(sta - t >= 0)
            def _(j=j):
                right_copy(sta - t, t - 1, j).wait_recv()

                @pl.when(has_right)
                def _():
                    right_copy(sta - t, t, j).start()

            @pl.when(sta + t < stas)
            def _(j=j):
                left_copy(sta + t, t - 1, j).wait_recv()

                @pl.when(has_left)
                def _():
                    left_copy(sta + t, t, j).start()
        return carry

    lax.fori_loop(1, stas, relay, 0)

    def drain(t, carry):
        for j in range(wins):
            @pl.when(has_right & (sta - t >= 0))
            def _(j=j):
                right_copy(sta - t, t, j).wait_send()

            @pl.when(has_left & (sta + t < stas))
            def _(j=j):
                left_copy(sta + t, t, j).wait_send()
        return carry

    lax.fori_loop(0, stas - 1, drain, 0)
    for hop in range(1, wins):
        win_copy(hop).wait_send()


def gathered_codes(x, table, local_wins):
    stas = lax.axis_size("sta")
    wins = lax.axis_size("win")
    cols = x.shape[0]
    lanes = cols // local_wins
    rows = BAND // wins * local_wins + 8
    dma = pltpu.SemaphoreType.DMA
    vmem = pl.BlockSpec(memory_space=pltpu.VMEM)
    return pl.pallas_call(
        functools.partial(spectra_kernel, stas, wins, local_wins),
        out_shape=jax.ShapeDtypeStruct((stas, wins, rows, lanes), jnp.int32),
        in_specs=[vmem, pl.BlockSpec(memory_space=pl.ANY)],
        out_specs=vmem,
        scratch_shapes=[
            pltpu.VMEM((4, 2, ROWS, PAD), jnp.bfloat16),
            pltpu.VMEM((cols, PAD), jnp.bfloat16),
            pltpu.VMEM((cols, PAD), jnp.bfloat16),
            pltpu.VMEM((2, ROWS, cols), jnp.float32),
            pltpu.VMEM((2, ROWS, cols), jnp.float32),
            pltpu.VMEM((2, ROWS, cols), jnp.float32),
            pltpu.VMEM((wins, rows, lanes), jnp.int32),
            dma((4,)), dma((2,)), dma((2,)), dma((wins,)), dma((wins,)),
            dma((stas, wins)), dma((stas, wins)), dma((stas, wins)), dma((stas, wins)), dma(()),
        ],
        compiler_params=pltpu.CompilerParams(
            collective_id=0, has_side_effects=True, vmem_limit_bytes=48 << 20
        ),
        name="spectra",
    )(x, table)


def pair_kernel(wins, local_wins, group, steps, slots_ref, left_ref, right_ref, out_ref):
    step = pl.program_id(1)
    lanes = left_ref.shape[-1]
    span = group * local_wins
    half = wins * span
    depth = 2 * half
    scale_row = left_ref.shape[2] - 8
    bins = out_ref.shape[1]
    factor = 1.0 / math.sqrt(wins * local_wins)

    def decoded(ref, first):
        planes = ([], [])
        for s in range(wins):
            word = ref[0, s, pl.ds(pl.multiple_of(first * local_wins, 8), span), :]
            odd = lax.broadcasted_iota(jnp.int32, (span, lanes), 0) % local_wins
            level = jnp.zeros((span, lanes), jnp.float32)
            for w in range(local_wins):
                unit = jnp.exp2(ref[0, s, scale_row + w:scale_row + w + 1, :].astype(jnp.float32) * 0.25)
                level = jnp.where(odd == w, unit * (1.0 / LEVELS), level)
            planes[0].append((word >> 16).astype(jnp.float32) * level)
            planes[1].append(((word << 16) >> 16).astype(jnp.float32) * level)
        return jnp.concatenate(planes[0], axis=0), jnp.concatenate(planes[1], axis=0)

    def turned(value):
        high = value.astype(jnp.bfloat16).astype(jnp.float32)
        both = jnp.concatenate([high, value - high], axis=0)
        return both.T.astype(jnp.bfloat16)

    row_bin = lax.broadcasted_iota(jnp.int32, (depth, 2 * lanes), 0) // local_wins % group
    col_odd = lax.broadcasted_iota(jnp.int32, (depth, 2 * lanes), 1) // lanes
    keep = row_bin % 2 == col_odd
    lane_pair = lax.broadcasted_iota(jnp.int32, (lanes, 2 * depth), 1) // local_wins % group // 2

    for g in range(bins // group):
        first = step * bins + g * group
        left_re, left_im = decoded(left_ref, first)
        right_re, right_im = decoded(right_ref, first)
        streams = (
            turned(jnp.concatenate([left_re, left_im], axis=0)),
            turned(jnp.concatenate([left_im, -left_re], axis=0)),
        )
        held = jnp.concatenate([right_re, right_im], axis=0)
        held = jnp.where(keep, jnp.concatenate([held, held], axis=1), 0.0)
        high, low = split(held)
        held = jnp.concatenate([high, high, low, low], axis=0)
        for m in range(group // 2):
            for p in range(2):
                part = jnp.where(lane_pair == m, streams[p], jnp.zeros_like(streams[p]))
                part = jnp.concatenate([part, part], axis=1)
                out = jnp.dot(part, held, preferred_element_type=jnp.float32) * factor
                out = out.astype(jnp.bfloat16)
                out_ref[0, g * group + 2 * m, p] = out[:, :lanes]
                out_ref[0, g * group + 2 * m + 1, p] = out[:, lanes:]


def pair_products(codes, slots, local_wins):
    stas, wins, rows, lanes = codes.shape
    bins = (rows - 8) // local_wins
    group = max(4, 64 // (2 * wins * local_wins))
    chunk = min(16, bins)
    count = slots.shape[0]
    spec = pltpu.PrefetchScalarGridSpec(
        num_scalar_prefetch=1,
        grid=(count, bins // chunk),
        in_specs=[
            pl.BlockSpec((1, wins, rows, lanes), lambda i, j, s: (s[i, 0], 0, 0, 0)),
            pl.BlockSpec((1, wins, rows, lanes), lambda i, j, s: (s[i, 1], 0, 0, 0)),
        ],
        out_specs=pl.BlockSpec((1, chunk, 2, lanes, lanes), lambda i, j, s: (i, j, 0, 0, 0)),
    )
    return pl.pallas_call(
        functools.partial(pair_kernel, wins, local_wins, group, bins // chunk),
        out_shape=jax.ShapeDtypeStruct((count, bins, 2, lanes, lanes), jnp.bfloat16),
        grid_spec=spec,
        compiler_params=pltpu.CompilerParams(vmem_limit_bytes=32 << 20),
        name="pairs",
    )(slots, codes, codes)


def local(table, records, valid_counts, pair_blocks):
    stations, local_wins, samples = records.shape
    freq = lax.axis_index("freq")
    index = freq * samples + jnp.arange(samples, dtype=jnp.int32)
    edge = SAMPLES // 20
    position = jnp.minimum(index, SAMPLES - 1 - index)
    ramp = 0.5 * (1.0 - jnp.cos(math.pi * (position.astype(jnp.float32) + 0.5) / edge))
    weight = jnp.where(position < edge, ramp, 1.0) / math.sqrt(SAMPLES)
    live = jnp.arange(stations, dtype=jnp.int32) < valid_counts[0]
    x = jnp.where(live[:, None, None], records * weight, 0.0)
    x = jnp.swapaxes(x, 0, 1).reshape(local_wins * stations, samples)
    x = jnp.pad(x, ((0, 0), (0, PAD - samples)))
    codes = gathered_codes(x, jnp.asarray(table), local_wins)
    slots = pair_blocks.shape[0] // lax.axis_size("sta")
    mine = lax.dynamic_slice_in_dim(pair_blocks, lax.axis_index("sta") * slots, slots, 0)
    return pair_products(codes, mine, local_wins)[:, None]


def solution(mesh):
    in_specs = (P(("group", "sta"), "win", "freq"), P(("group", "sta")), P("group", None))
    out_specs = P(("group", "sta"), "freq", "win", None, None, None)
    body = functools.partial(local, dft_table())
    return jax.shard_map(body, mesh=mesh, in_specs=in_specs, out_specs=out_specs, check_vma=False)
```

```python
import functools
import math

import jax
import jax.numpy as jnp
import numpy as np
from jax import lax
from jax.experimental import pallas as pl
from jax.experimental.pallas import tpu as pltpu
from jax.sharding import PartitionSpec as P

SAMPLES = 3600
BINS = 512
HALF_WIDTH = 10
AMP_FLOOR = 0.1
HALO = 16
PAD = 1920
BAND = BINS // 2
ROWS = BAND + HALO
LEVELS = 32766.0
MESH = pl.DeviceIdType.MESH


def band_bins(band):
    own = np.arange(BAND) + band * BAND
    halo = np.arange(HALO) + (BAND if band == 0 else BAND - HALO)
    return np.concatenate([own, halo])


def dft_table():
    half = SAMPLES // 2
    table = np.zeros((2, 2, 2, ROWS, PAD), jnp.bfloat16)
    for band in range(2):
        phase = (band_bins(band)[:, None] + 1) * np.arange(half)[None] % SAMPLES
        angle = phase * (2.0 * math.pi / SAMPLES)
        for part, wave in enumerate((np.cos(angle), -np.sin(angle))):
            value = wave / math.sqrt(SAMPLES)
            high = value.astype(jnp.bfloat16)
            table[band, part, 0, :, :half] = high
            table[band, part, 1, :, :half] = (value - high.astype(np.float64)).astype(jnp.bfloat16)
    return table


def split(value):
    high = value.astype(jnp.bfloat16)
    return high, (value - high.astype(jnp.float32)).astype(jnp.bfloat16)


def dot(a, b):
    return jnp.dot(a, b, preferred_element_type=jnp.float32)


def spectra_kernel(
    stas, wins, local_wins, live_ref, x_ref, table_ref, out_ref,
    tab, raw, xh, xl, give, got, own, codes,
    tab_sem, raw_sem, fs_sem, fr_sem, ws_sem, wr_sem, rs_sem, rr_sem, ls_sem, lr_sem, own_sem,
):
    sta = lax.axis_index("sta")
    win = lax.axis_index("win")
    freq = lax.axis_index("freq")
    other = 1 - freq
    samples, lanes = x_ref.shape[1:]
    sub = BAND // wins
    has_right = sta < stas - 1
    has_left = sta > 0

    def table_copy(step):
        band = other if step < 2 else freq
        return pltpu.make_async_copy(
            table_ref.at[band, step % 2], tab.at[step], tab_sem.at[step]
        )

    raw_copy = pltpu.make_async_copy(x_ref, raw, raw_sem)
    raw_copy.start()
    for step in range(4):
        table_copy(step).start()

    barrier = pltpu.get_barrier_semaphore()
    pl.semaphore_signal(barrier, inc=1, device_id={"freq": other}, device_id_type=MESH)
    for hop in range(1, wins):
        pl.semaphore_signal(
            barrier, inc=1, device_id={"win": lax.rem(win + hop, wins)}, device_id_type=MESH
        )

    @pl.when(has_right)
    def _():
        pl.semaphore_signal(barrier, inc=1, device_id={"sta": sta + 1}, device_id_type=MESH)

    @pl.when(has_left)
    def _():
        pl.semaphore_signal(barrier, inc=1, device_id={"sta": sta - 1}, device_id_type=MESH)

    edge = SAMPLES // 20
    span = -(-edge // 8) * 8
    begin = pl.multiple_of(freq * (samples - span), 8)
    at = begin + lax.broadcasted_iota(jnp.int32, (span, lanes), 0)
    position = jnp.where(freq == 0, at, samples - 1 - at)
    ramp = 0.5 * (1.0 - jnp.cos(math.pi * (position.astype(jnp.float32) + 0.5) / edge))
    ramp = jnp.where(position < edge, ramp, 1.0)
    raw_copy.wait()
    for w in range(local_wins):
        part = slice(w * lanes, (w + 1) * lanes)
        raw[w, pl.ds(begin, span), :] = raw[w, pl.ds(begin, span), :] * ramp
        high, low = split(raw[w])
        xh[:samples, part] = high
        xl[:samples, part] = low
    blank = jnp.zeros((PAD - samples, local_wins * lanes), jnp.bfloat16)
    xh[samples:] = blank
    xl[samples:] = blank

    ends = jnp.where(has_right, 1, 0) + jnp.where(has_left, 1, 0)
    pl.semaphore_wait(barrier, wins + ends)

    odd = lax.broadcasted_iota(jnp.int32, (ROWS, 1), 0) % 2
    sign = jnp.where((odd == 0) & (freq == 1), -1.0, 1.0).astype(jnp.float32)

    def partial(step):
        table_copy(step).wait()
        value = dot(tab[step, 0], xh[...]) + (
            dot(tab[step, 0], xl[...]) + dot(tab[step, 1], xh[...])
        )
        return value * sign

    def freq_copy(step):
        return pltpu.make_async_remote_copy(
            src_ref=give.at[step], dst_ref=got.at[step],
            send_sem=fs_sem.at[step], recv_sem=fr_sem.at[step],
            device_id={"freq": other}, device_id_type=MESH,
        )

    for step in range(2):
        give[step] = partial(step)
        freq_copy(step).start()
    for step in range(2):
        own[step] = partial(2 + step)
    for step in range(2):
        freq_copy(step).wait()

    real = own[0] + got[0]
    imag = own[1] + got[1]
    magnitude = jnp.sqrt(real * real + imag * imag)
    row = lax.broadcasted_iota(jnp.int32, (BAND, ROWS), 0)
    col = lax.broadcasted_iota(jnp.int32, (BAND, ROWS), 1)
    place = jnp.where(col < BAND, col, jnp.where(freq == 0, col, col - BAND - HALO))
    box = ((place - row <= HALF_WIDTH) & (row - place <= HALF_WIDTH)).astype(jnp.float32)
    box = box.astype(jnp.bfloat16)
    mag_high, mag_low = split(magnitude)
    summed = jnp.dot(box, mag_high, preferred_element_type=jnp.float32) + jnp.dot(
        box, mag_low, preferred_element_type=jnp.float32
    )
    bin_at = freq * BAND + lax.broadcasted_iota(jnp.int32, (BAND, 1), 0)
    counted = (
        jnp.minimum(bin_at + HALF_WIDTH, BINS - 1) - jnp.maximum(bin_at - HALF_WIDTH, 0) + 1
    ).astype(jnp.float32)
    station = lax.broadcasted_iota(jnp.int32, (1, local_wins * lanes), 1) % lanes
    live = (station < live_ref[0]).astype(jnp.float32)
    inverse = live / jnp.maximum(summed / counted, AMP_FLOOR)
    real = real[:BAND] * inverse
    imag = imag[:BAND] * inverse

    for dest in range(wins):
        for w in range(local_wins):
            re = real[dest * sub:(dest + 1) * sub, w * lanes:(w + 1) * lanes]
            im = imag[dest * sub:(dest + 1) * sub, w * lanes:(w + 1) * lanes]
            peak = jnp.max(jnp.maximum(jnp.abs(re), jnp.abs(im)), axis=0, keepdims=True)
            level = jnp.ceil(jnp.log2(jnp.maximum(peak, 1e-30)) * 4.0 + 0.01)
            factor = jnp.exp2(level * -0.25) * LEVELS
            top = jnp.round(re * factor).astype(jnp.int32)
            bottom = jnp.round(im * factor).astype(jnp.int32)
            codes[dest, pl.ds(w, sub, stride=local_wins), :] = top * 65536 + (bottom & 65535)
            codes[dest, pl.ds(sub * local_wins + w, 1), :] = level.astype(jnp.int32)

    def win_copy(hop):
        to = lax.rem(win + hop, wins)
        return pltpu.make_async_remote_copy(
            src_ref=codes.at[to], dst_ref=out_ref.at[sta, win],
            send_sem=ws_sem.at[hop], recv_sem=wr_sem.at[hop],
            device_id={"win": to}, device_id_type=MESH,
        )

    for hop in range(1, wins):
        win_copy(hop).start()
    keep = pltpu.make_async_copy(codes.at[win], out_ref.at[sta, win], own_sem)
    keep.start()
    keep.wait()

    def slot(block, j):
        return out_ref.at[block, lax.rem(win - j + wins, wins)]

    def right_copy(block, t, j):
        return pltpu.make_async_remote_copy(
            src_ref=slot(block, j), dst_ref=slot(block, j),
            send_sem=rs_sem.at[t, j], recv_sem=rr_sem.at[t, j],
            device_id={"sta": sta + 1}, device_id_type=MESH,
        )

    def left_copy(block, t, j):
        return pltpu.make_async_remote_copy(
            src_ref=slot(block, j), dst_ref=slot(block, j),
            send_sem=ls_sem.at[t, j], recv_sem=lr_sem.at[t, j],
            device_id={"sta": sta - 1}, device_id_type=MESH,
        )

    for j in range(wins):
        if j > 0:
            win_copy(j).wait_recv()

        @pl.when(has_right)
        def _(j=j):
            right_copy(sta, 0, j).start()

        @pl.when(has_left)
        def _(j=j):
            left_copy(sta, 0, j).start()

    def relay(t, carry):
        for j in range(wins):
            @pl.when(sta - t >= 0)
            def _(j=j):
                right_copy(sta - t, t - 1, j).wait_recv()

                @pl.when(has_right)
                def _():
                    right_copy(sta - t, t, j).start()

            @pl.when(sta + t < stas)
            def _(j=j):
                left_copy(sta + t, t - 1, j).wait_recv()

                @pl.when(has_left)
                def _():
                    left_copy(sta + t, t, j).start()
        return carry

    lax.fori_loop(1, stas, relay, 0)

    def drain(t, carry):
        for j in range(wins):
            @pl.when(has_right & (sta - t >= 0))
            def _(j=j):
                right_copy(sta - t, t, j).wait_send()

            @pl.when(has_left & (sta + t < stas))
            def _(j=j):
                left_copy(sta + t, t, j).wait_send()
        return carry

    lax.fori_loop(0, stas - 1, drain, 0)
    for hop in range(1, wins):
        win_copy(hop).wait_send()


def gathered_codes(live, x, table):
    stas = lax.axis_size("sta")
    wins = lax.axis_size("win")
    local_wins, samples, lanes = x.shape
    cols = local_wins * lanes
    rows = BAND // wins * local_wins + 8
    dma = pltpu.SemaphoreType.DMA
    hold = pl.BlockSpec(memory_space=pl.ANY)
    return pl.pallas_call(
        functools.partial(spectra_kernel, stas, wins, local_wins),
        out_shape=jax.ShapeDtypeStruct((stas, wins, rows, lanes), jnp.int32),
        in_specs=[pl.BlockSpec(memory_space=pltpu.SMEM), hold, hold],
        out_specs=pl.BlockSpec(memory_space=pltpu.VMEM),
        scratch_shapes=[
            pltpu.VMEM((4, 2, ROWS, PAD), jnp.bfloat16),
            pltpu.VMEM((local_wins, samples, lanes), jnp.float32),
            pltpu.VMEM((PAD, cols), jnp.bfloat16),
            pltpu.VMEM((PAD, cols), jnp.bfloat16),
            pltpu.VMEM((2, ROWS, cols), jnp.float32),
            pltpu.VMEM((2, ROWS, cols), jnp.float32),
            pltpu.VMEM((2, ROWS, cols), jnp.float32),
            pltpu.VMEM((wins, rows, lanes), jnp.int32),
            dma((4,)), dma(()), dma((2,)), dma((2,)), dma((wins,)), dma((wins,)),
            dma((stas, wins)), dma((stas, wins)), dma((stas, wins)), dma((stas, wins)), dma(()),
        ],
        compiler_params=pltpu.CompilerParams(
            collective_id=0, has_side_effects=True, vmem_limit_bytes=61 << 20
        ),
        name="spectra",
    )(live, x, table)


def pair_kernel(wins, local_wins, group, steps, slots_ref, left_ref, right_ref, out_ref):
    step = pl.program_id(1)
    lanes = left_ref.shape[-1]
    span = group * local_wins
    half = wins * span
    depth = 2 * half
    scale_row = left_ref.shape[2] - 8
    bins = out_ref.shape[1]
    factor = 1.0 / math.sqrt(wins * local_wins)

    odd = lax.broadcasted_iota(jnp.int32, (span, lanes), 0) % local_wins

    def levels(ref, scale):
        found = []
        for s in range(wins):
            level = jnp.zeros((span, lanes), jnp.float32)
            for w in range(local_wins):
                row = ref[0, s, scale_row + w:scale_row + w + 1, :].astype(jnp.float32)
                level = jnp.where(odd == w, jnp.exp2(row * 0.25) * scale, level)
            found.append(level)
        return found

    left_levels = levels(left_ref, 1.0 / LEVELS)
    right_levels = levels(right_ref, factor / LEVELS)

    def decoded(ref, first, found):
        planes = ([], [])
        for s in range(wins):
            word = ref[0, s, pl.ds(pl.multiple_of(first * local_wins, 8), span), :]
            level = found[s]
            planes[0].append((word >> 16).astype(jnp.float32) * level)
            planes[1].append(((word << 16) >> 16).astype(jnp.float32) * level)
        return jnp.concatenate(planes[0], axis=0), jnp.concatenate(planes[1], axis=0)

    def turned(value):
        high = value.astype(jnp.bfloat16).astype(jnp.float32)
        both = jnp.concatenate([high, value - high], axis=0)
        return both.T.astype(jnp.bfloat16)

    row_bin = lax.broadcasted_iota(jnp.int32, (depth, 2 * lanes), 0) // local_wins % group
    col_odd = lax.broadcasted_iota(jnp.int32, (depth, 2 * lanes), 1) // lanes
    keep = row_bin % 2 == col_odd
    lane_pair = lax.broadcasted_iota(jnp.int32, (lanes, 2 * depth), 1) // local_wins % group // 2

    for g in range(bins // group):
        first = step * bins + g * group
        left_re, left_im = decoded(left_ref, first, left_levels)
        right_re, right_im = decoded(right_ref, first, right_levels)
        streams = (
            turned(jnp.concatenate([left_re, left_im], axis=0)),
            turned(jnp.concatenate([left_im, -left_re], axis=0)),
        )
        held = jnp.concatenate([right_re, right_im], axis=0)
        held = jnp.where(keep, jnp.concatenate([held, held], axis=1), 0.0)
        high, low = split(held)
        held = jnp.concatenate([high, high, low, low], axis=0)
        for m in range(group // 2):
            for p in range(2):
                part = jnp.where(lane_pair == m, streams[p], jnp.zeros_like(streams[p]))
                part = jnp.concatenate([part, part], axis=1)
                out = jnp.dot(part, held, preferred_element_type=jnp.float32)
                out = out.astype(jnp.bfloat16)
                out_ref[0, g * group + 2 * m, p] = out[:, :lanes]
                out_ref[0, g * group + 2 * m + 1, p] = out[:, lanes:]


def pair_products(codes, slots, local_wins):
    stas, wins, rows, lanes = codes.shape
    bins = (rows - 8) // local_wins
    group = max(4, 64 // (2 * wins * local_wins))
    chunk = min(32, bins)
    count = slots.shape[0]
    spec = pltpu.PrefetchScalarGridSpec(
        num_scalar_prefetch=1,
        grid=(count, bins // chunk),
        in_specs=[
            pl.BlockSpec((1, wins, rows, lanes), lambda i, j, s: (s[i, 0], 0, 0, 0)),
            pl.BlockSpec((1, wins, rows, lanes), lambda i, j, s: (s[i, 1], 0, 0, 0)),
        ],
        out_specs=pl.BlockSpec((1, chunk, 2, lanes, lanes), lambda i, j, s: (i, j, 0, 0, 0)),
    )
    return pl.pallas_call(
        functools.partial(pair_kernel, wins, local_wins, group, bins // chunk),
        out_shape=jax.ShapeDtypeStruct((count, bins, 2, lanes, lanes), jnp.bfloat16),
        grid_spec=spec,
        compiler_params=pltpu.CompilerParams(vmem_limit_bytes=32 << 20),
        name="pairs",
    )(slots, codes, codes)


def local(table, records, valid_counts, pair_blocks):
    local_wins = records.shape[1]
    codes = gathered_codes(valid_counts, jnp.transpose(records, (1, 2, 0)), jnp.asarray(table))
    slots = pair_blocks.shape[0] // lax.axis_size("sta")
    mine = lax.dynamic_slice_in_dim(pair_blocks, lax.axis_index("sta") * slots, slots, 0)
    return pair_products(codes, mine, local_wins)[:, None]


def solution(mesh):
    in_specs = (P(("group", "sta"), "win", "freq"), P(("group", "sta")), P("group", None))
    out_specs = P(("group", "sta"), "freq", "win", None, None, None)
    body = functools.partial(local, dft_table())
    return jax.shard_map(body, mesh=mesh, in_specs=in_specs, out_specs=out_specs, check_vma=False)
```

```python
import functools
import math

import jax
import jax.numpy as jnp
import numpy as np
from jax import lax
from jax.experimental import pallas as pl
from jax.experimental.pallas import tpu as pltpu
from jax.sharding import PartitionSpec as P

SAMPLES = 3600
BINS = 512
HALF_WIDTH = 10
AMP_FLOOR = 0.1
HALO = 16
PAD = 1920
BAND = BINS // 2
ROWS = BAND + HALO
LEVELS = 32766.0
MESH = pl.DeviceIdType.MESH


def dft_table():
    half = SAMPLES // 2
    table = np.zeros((2, 2, 2, ROWS, PAD), jnp.bfloat16)
    for band in range(2):
        bins = np.arange(ROWS) + band * (BAND - HALO)
        phase = (bins[:, None] + 1) * np.arange(half)[None] % SAMPLES
        angle = phase * (2.0 * math.pi / SAMPLES)
        for part, wave in enumerate((np.cos(angle), -np.sin(angle))):
            value = wave / math.sqrt(SAMPLES)
            high = value.astype(jnp.bfloat16)
            table[band, 0, part, :, :half] = high
            table[band, 1, part, :, :half] = (value - high.astype(np.float64)).astype(jnp.bfloat16)
    return table


def split(value):
    high = value.astype(jnp.bfloat16)
    return high, (value - high.astype(jnp.float32)).astype(jnp.bfloat16)


def dot(a, b):
    return jnp.dot(a, b, preferred_element_type=jnp.float32)


def chunk_rows(wins):
    first = BAND // 2 + 2 * HALO if wins == 2 else ROWS
    return (first, ROWS - first) if first < ROWS else (first,)


def spectra_kernel(
    stas, wins, local_wins, live_ref, x_ref, table_ref, out_ref,
    raw, xh, xl, spec, mag, codes,
    raw_sem, tab_sem, fs_sem, fr_sem, ws_sem, wr_sem, rs_sem, rr_sem, ls_sem, lr_sem, own_sem,
    *chunks,
):
    sta = lax.axis_index("sta")
    win = lax.axis_index("win")
    freq = lax.axis_index("freq")
    other = 1 - freq
    samples, lanes = x_ref.shape[1:]
    cols = local_wins * lanes
    sub = BAND // wins
    has_right = sta < stas - 1
    has_left = sta > 0
    sizes = chunk_rows(wins)
    if len(sizes) == 2:
        starts = (win * sizes[1], (1 - win) * sizes[0])
    else:
        starts = (0,)
    tabs, gives, gots = chunks[0::3], chunks[1::3], chunks[2::3]

    def table_copy(c, mine):
        rows = pl.ds(pl.multiple_of(starts[c], 16), sizes[c])
        return pltpu.make_async_copy(
            table_ref.at[freq if mine else other, :, :, rows, :], tabs[c].at[mine],
            tab_sem.at[c, mine],
        )

    raw_copy = pltpu.make_async_copy(x_ref, raw, raw_sem)
    raw_copy.start()
    for c in range(len(sizes)):
        for mine in range(2):
            table_copy(c, mine).start()

    barrier = pltpu.get_barrier_semaphore()
    pl.semaphore_signal(barrier, inc=1, device_id={"freq": other}, device_id_type=MESH)
    for hop in range(1, wins):
        pl.semaphore_signal(
            barrier, inc=1, device_id={"win": lax.rem(win + hop, wins)}, device_id_type=MESH
        )

    @pl.when(has_right)
    def _():
        pl.semaphore_signal(barrier, inc=1, device_id={"sta": sta + 1}, device_id_type=MESH)

    @pl.when(has_left)
    def _():
        pl.semaphore_signal(barrier, inc=1, device_id={"sta": sta - 1}, device_id_type=MESH)

    edge = SAMPLES // 20
    span = -(-edge // 8) * 8
    begin = pl.multiple_of(freq * (samples - span), 8)
    at = begin + lax.broadcasted_iota(jnp.int32, (span, lanes), 0)
    position = jnp.where(freq == 0, at, samples - 1 - at)
    ramp = 0.5 * (1.0 - jnp.cos(math.pi * (position.astype(jnp.float32) + 0.5) / edge))
    ramp = jnp.where(position < edge, ramp, 1.0)
    raw_copy.wait()
    for w in range(local_wins):
        part = slice(w * lanes, (w + 1) * lanes)
        raw[w, pl.ds(begin, span), :] = raw[w, pl.ds(begin, span), :] * ramp
        high, low = split(raw[w])
        xh[:samples, part] = high
        xl[:samples, part] = low
    blank = jnp.zeros((PAD - samples, cols), jnp.bfloat16)
    xh[samples:] = blank
    xl[samples:] = blank

    ends = jnp.where(has_right, 1, 0) + jnp.where(has_left, 1, 0)
    pl.semaphore_wait(barrier, wins + ends)

    def partial(c, mine):
        rows = sizes[c]
        table_copy(c, mine).wait()
        odd = lax.broadcasted_iota(jnp.int32, (2 * rows, 1), 0) % 2
        sign = jnp.where((odd == 0) & (freq == 1), -1.0, 1.0).astype(jnp.float32)
        both = dot(tabs[c][mine].reshape(4 * rows, PAD), xh[...])
        rest = dot(tabs[c][mine, 0].reshape(2 * rows, PAD), xl[...])
        value = (both[:2 * rows] + (both[2 * rows:] + rest)) * sign
        return value.reshape(2, rows, cols)

    def freq_copy(c):
        return pltpu.make_async_remote_copy(
            src_ref=gives[c], dst_ref=gots[c],
            send_sem=fs_sem.at[c], recv_sem=fr_sem.at[c],
            device_id={"freq": other}, device_id_type=MESH,
        )

    def transform(c, between=None):
        rows = pl.ds(pl.multiple_of(starts[c], 16), sizes[c])
        gives[c][...] = partial(c, 0)
        freq_copy(c).start()
        value = partial(c, 1)
        if between is not None:
            between()
        freq_copy(c).wait_recv()
        value = value + gots[c][...]
        spec[:, rows, :] = value
        mag[rows, :] = jnp.sqrt(value[0] * value[0] + value[1] * value[1])

    station = lax.broadcasted_iota(jnp.int32, (1, cols), 1) % lanes
    live = (station < live_ref[0]).astype(jnp.float32)

    def encode(hop, start, count):
        dest = lax.rem(win + hop, wins)
        bin_at = freq * BAND + dest * sub + lax.broadcasted_iota(jnp.int32, (sub, count), 0)
        near = start + freq * (BAND - HALO) + lax.broadcasted_iota(jnp.int32, (sub, count), 1)
        box = (near - bin_at <= HALF_WIDTH) & (bin_at - near <= HALF_WIDTH)
        box = box.astype(jnp.float32).astype(jnp.bfloat16)
        high, low = split(mag[pl.ds(pl.multiple_of(start, 16), count), :])
        summed = dot(box, high) + dot(box, low)
        bin_at = freq * BAND + dest * sub + lax.broadcasted_iota(jnp.int32, (sub, 1), 0)
        counted = (
            jnp.minimum(bin_at + HALF_WIDTH, BINS - 1) - jnp.maximum(bin_at - HALF_WIDTH, 0) + 1
        ).astype(jnp.float32)
        inverse = live / jnp.maximum(summed / counted, AMP_FLOOR)
        rows = pl.ds(pl.multiple_of(freq * HALO + dest * sub, 16), sub)
        real = spec[0, rows, :] * inverse
        imag = spec[1, rows, :] * inverse
        for w in range(local_wins):
            re = real[:, w * lanes:(w + 1) * lanes]
            im = imag[:, w * lanes:(w + 1) * lanes]
            peak = jnp.max(jnp.maximum(jnp.abs(re), jnp.abs(im)), axis=0, keepdims=True)
            level = jnp.ceil(jnp.log2(jnp.maximum(peak, 1e-30)) * 4.0 + 0.01)
            factor = jnp.exp2(level * -0.25) * LEVELS
            top = jnp.round(re * factor).astype(jnp.int32)
            bottom = jnp.round(im * factor).astype(jnp.int32)
            codes[hop, pl.ds(w, sub, stride=local_wins), :] = top * 65536 + (bottom & 65535)
            codes[hop, pl.ds(sub * local_wins + w, 1), :] = level.astype(jnp.int32)

    def win_copy(hop):
        return pltpu.make_async_remote_copy(
            src_ref=codes.at[hop], dst_ref=out_ref.at[sta, win],
            send_sem=ws_sem.at[hop], recv_sem=wr_sem.at[hop],
            device_id={"win": lax.rem(win + hop, wins)}, device_id_type=MESH,
        )

    def slot(block, j):
        return out_ref.at[block, lax.rem(win - j + wins, wins)]

    def right_copy(block, t, j, own=False):
        return pltpu.make_async_remote_copy(
            src_ref=codes.at[0] if own else slot(block, j), dst_ref=slot(block, j),
            send_sem=rs_sem.at[t, j], recv_sem=rr_sem.at[t, j],
            device_id={"sta": sta + 1}, device_id_type=MESH,
        )

    def left_copy(block, t, j, own=False):
        return pltpu.make_async_remote_copy(
            src_ref=codes.at[0] if own else slot(block, j), dst_ref=slot(block, j),
            send_sem=ls_sem.at[t, j], recv_sem=lr_sem.at[t, j],
            device_id={"sta": sta - 1}, device_id_type=MESH,
        )

    def depart(j):
        @pl.when(has_right)
        def _():
            right_copy(sta, 0, j, j == 0).start()

        @pl.when(has_left)
        def _():
            left_copy(sta, 0, j, j == 0).start()

    def relay(low, high, j):
        def step(t, carry):
            @pl.when(sta - t >= 0)
            def _():
                right_copy(sta - t, t - 1, j).wait_recv()

                @pl.when(has_right)
                def _():
                    right_copy(sta - t, t, j).start()

            @pl.when(sta + t < stas)
            def _():
                left_copy(sta + t, t - 1, j).wait_recv()

                @pl.when(has_left)
                def _():
                    left_copy(sta + t, t, j).start()

            return carry

        lax.fori_loop(low, high, step, 0)

    transform(0)
    encode(0, starts[0], sizes[0])
    depart(0)
    keep = pltpu.make_async_copy(codes.at[0], out_ref.at[sta, win], own_sem)
    keep.start()
    early = min(2, stas)
    if len(sizes) == 2:
        transform(1, lambda: relay(1, early, 0))
    for hop in range(1, wins):
        encode(hop, 0, ROWS)
        win_copy(hop).start()
    if len(sizes) == 1:
        relay(1, early, 0)
    late = min(3, stas)
    relay(early, late, 0)
    for j in range(1, wins):
        win_copy(j).wait_recv()
        depart(j)
    relay(late, stas, 0)
    for j in range(1, wins):
        relay(1, stas, j)

    def drain(t, carry):
        for j in range(wins):
            @pl.when(has_right & (sta - t >= 0))
            def _(j=j):
                right_copy(sta - t, t, j).wait_send()

            @pl.when(has_left & (sta + t < stas))
            def _(j=j):
                left_copy(sta + t, t, j).wait_send()
        return carry

    lax.fori_loop(0, stas - 1, drain, 0)
    for c in range(len(sizes)):
        freq_copy(c).wait_send()
    for hop in range(1, wins):
        win_copy(hop).wait_send()
    keep.wait()


def gathered_codes(live, x, table):
    stas = lax.axis_size("sta")
    wins = lax.axis_size("win")
    local_wins, samples, lanes = x.shape
    cols = local_wins * lanes
    rows = BAND // wins * local_wins + 8
    dma = pltpu.SemaphoreType.DMA
    chunks = []
    for size in chunk_rows(wins):
        chunks.append(pltpu.VMEM((2, 2, 2, size, PAD), jnp.bfloat16))
        chunks += [pltpu.VMEM((2, size, cols), jnp.float32)] * 2
    hold = pl.BlockSpec(memory_space=pl.ANY)
    return pl.pallas_call(
        functools.partial(spectra_kernel, stas, wins, local_wins),
        out_shape=jax.ShapeDtypeStruct((stas, wins, rows, lanes), jnp.int32),
        in_specs=[pl.BlockSpec(memory_space=pltpu.SMEM), hold, hold],
        out_specs=pl.BlockSpec(memory_space=pltpu.VMEM),
        scratch_shapes=[
            pltpu.VMEM((local_wins, samples, lanes), jnp.float32),
            pltpu.VMEM((PAD, cols), jnp.bfloat16),
            pltpu.VMEM((PAD, cols), jnp.bfloat16),
            pltpu.VMEM((2, ROWS, cols), jnp.float32),
            pltpu.VMEM((ROWS, cols), jnp.float32),
            pltpu.VMEM((wins, rows, lanes), jnp.int32),
            dma(()), dma((2, 2)), dma((2,)), dma((2,)), dma((wins,)), dma((wins,)),
            dma((stas, wins)), dma((stas, wins)), dma((stas, wins)), dma((stas, wins)), dma(()),
        ] + chunks,
        compiler_params=pltpu.CompilerParams(
            collective_id=0, has_side_effects=True, vmem_limit_bytes=62 << 20
        ),
        name="spectra",
    )(live, x, table)


def pair_kernel(wins, local_wins, group, steps, slots_ref, left_ref, right_ref, out_ref):
    step = pl.program_id(1)
    lanes = left_ref.shape[-1]
    span = group * local_wins
    half = wins * span
    depth = 2 * half
    scale_row = left_ref.shape[2] - 8
    bins = out_ref.shape[1]
    factor = 1.0 / math.sqrt(wins * local_wins)

    odd = lax.broadcasted_iota(jnp.int32, (span, lanes), 0) % local_wins

    def levels(ref, scale):
        found = []
        for s in range(wins):
            level = jnp.zeros((span, lanes), jnp.float32)
            for w in range(local_wins):
                row = ref[0, s, scale_row + w:scale_row + w + 1, :].astype(jnp.float32)
                level = jnp.where(odd == w, jnp.exp2(row * 0.25) * scale, level)
            found.append(level)
        return found

    left_levels = levels(left_ref, 1.0 / LEVELS)
    right_levels = levels(right_ref, factor / LEVELS)

    def decoded(ref, first, found):
        planes = ([], [])
        for s in range(wins):
            word = ref[0, s, pl.ds(pl.multiple_of(first * local_wins, 8), span), :]
            level = found[s]
            planes[0].append((word >> 16).astype(jnp.float32) * level)
            planes[1].append(((word << 16) >> 16).astype(jnp.float32) * level)
        return jnp.concatenate(planes[0], axis=0), jnp.concatenate(planes[1], axis=0)

    def turned(value):
        high = value.astype(jnp.bfloat16).astype(jnp.float32)
        both = jnp.concatenate([high, value - high], axis=0)
        return both.T.astype(jnp.bfloat16)

    row_bin = lax.broadcasted_iota(jnp.int32, (depth, 2 * lanes), 0) // local_wins % group
    col_odd = lax.broadcasted_iota(jnp.int32, (depth, 2 * lanes), 1) // lanes
    keep = row_bin % 2 == col_odd
    lane_pair = lax.broadcasted_iota(jnp.int32, (lanes, 2 * depth), 1) // local_wins % group // 2

    for g in range(bins // group):
        first = step * bins + g * group
        left_re, left_im = decoded(left_ref, first, left_levels)
        right_re, right_im = decoded(right_ref, first, right_levels)
        streams = (
            turned(jnp.concatenate([left_re, left_im], axis=0)),
            turned(jnp.concatenate([left_im, -left_re], axis=0)),
        )
        held = jnp.concatenate([right_re, right_im], axis=0)
        held = jnp.where(keep, jnp.concatenate([held, held], axis=1), 0.0)
        high, low = split(held)
        held = jnp.concatenate([high, high, low, low], axis=0)
        for m in range(group // 2):
            for p in range(2):
                part = jnp.where(lane_pair == m, streams[p], jnp.zeros_like(streams[p]))
                part = jnp.concatenate([part, part], axis=1)
                out = jnp.dot(part, held, preferred_element_type=jnp.float32)
                out = out.astype(jnp.bfloat16)
                out_ref[0, g * group + 2 * m, p] = out[:, :lanes]
                out_ref[0, g * group + 2 * m + 1, p] = out[:, lanes:]


def pair_products(codes, slots, local_wins):
    stas, wins, rows, lanes = codes.shape
    bins = (rows - 8) // local_wins
    group = max(4, 64 // (2 * wins * local_wins))
    chunk = min(32, bins)
    count = slots.shape[0]
    spec = pltpu.PrefetchScalarGridSpec(
        num_scalar_prefetch=1,
        grid=(count, bins // chunk),
        in_specs=[
            pl.BlockSpec((1, wins, rows, lanes), lambda i, j, s: (s[i, 0], 0, 0, 0)),
            pl.BlockSpec((1, wins, rows, lanes), lambda i, j, s: (s[i, 1], 0, 0, 0)),
        ],
        out_specs=pl.BlockSpec((1, chunk, 2, lanes, lanes), lambda i, j, s: (i, j, 0, 0, 0)),
    )
    return pl.pallas_call(
        functools.partial(pair_kernel, wins, local_wins, group, bins // chunk),
        out_shape=jax.ShapeDtypeStruct((count, bins, 2, lanes, lanes), jnp.bfloat16),
        grid_spec=spec,
        compiler_params=pltpu.CompilerParams(vmem_limit_bytes=62 << 20),
        name="pairs",
    )(slots, codes, codes)


def local(table, records, valid_counts, pair_blocks):
    local_wins = records.shape[1]
    codes = gathered_codes(valid_counts, jnp.transpose(records, (1, 2, 0)), jnp.asarray(table))
    slots = pair_blocks.shape[0] // lax.axis_size("sta")
    mine = lax.dynamic_slice_in_dim(pair_blocks, lax.axis_index("sta") * slots, slots, 0)
    return pair_products(codes, mine, local_wins)[:, None]


def solution(mesh):
    in_specs = (P(("group", "sta"), "win", "freq"), P(("group", "sta")), P("group", None))
    out_specs = P(("group", "sta"), "freq", "win", None, None, None)
    body = functools.partial(local, dft_table())
    return jax.shard_map(body, mesh=mesh, in_specs=in_specs, out_specs=out_specs, check_vma=False)
```

```python
import functools
import math

import jax
import jax.numpy as jnp
import numpy as np
from jax import lax
from jax.experimental import pallas as pl
from jax.experimental.pallas import tpu as pltpu
from jax.sharding import PartitionSpec as P

SAMPLES = 3600
BINS = 512
HALF_WIDTH = 10
AMP_FLOOR = 0.1
HALO = 16
PAD = 1920
BAND = BINS // 2
ROWS = BAND + HALO
LEVELS = 32766.0
MESH = pl.DeviceIdType.MESH


def dft_factors():
    table = np.zeros((2, 2, 2, ROWS, 128), np.float32)
    for band in range(2):
        bins = np.arange(ROWS)[:, None] + band * (BAND - HALO) + 1
        base = bins * np.arange(128)[None] % SAMPLES * (2.0 * math.pi / SAMPLES)
        turn = bins * 128 * np.arange(128)[None] % SAMPLES * (2.0 * math.pi / SAMPLES)
        table[band, 0, 0] = np.cos(base) / math.sqrt(SAMPLES)
        table[band, 0, 1] = -np.sin(base) / math.sqrt(SAMPLES)
        table[band, 1, 0] = np.cos(turn)
        table[band, 1, 1] = np.sin(turn)
    return table


def split(value):
    high = value.astype(jnp.bfloat16)
    return high, (value - high.astype(jnp.float32)).astype(jnp.bfloat16)


def dot(a, b):
    return jnp.dot(a, b, preferred_element_type=jnp.float32)


def chunk_rows(wins):
    first = BAND // 2 + 2 * HALO if wins == 2 else ROWS
    return (first, ROWS - first) if first < ROWS else (first,)


def spectra_kernel(
    stas, wins, local_wins, live_ref, x_ref, table_ref, out_ref,
    raw, xh, xl, spec, mag, codes,
    raw_sem, fs_sem, fr_sem, ws_sem, wr_sem, rs_sem, rr_sem, ls_sem, lr_sem, own_sem,
    *chunks,
):
    sta = lax.axis_index("sta")
    win = lax.axis_index("win")
    freq = lax.axis_index("freq")
    other = 1 - freq
    samples, lanes = x_ref.shape[1:]
    cols = local_wins * lanes
    sub = BAND // wins
    has_right = sta < stas - 1
    has_left = sta > 0
    sizes = chunk_rows(wins)
    if len(sizes) == 2:
        starts = (win * sizes[1], (1 - win) * sizes[0])
    else:
        starts = (0,)
    tabs, gives, gots = chunks[0::3], chunks[1::3], chunks[2::3]

    def fill(c, mine):
        rows = pl.ds(pl.multiple_of(starts[c], 16), sizes[c])
        band = freq if mine else other
        base_cos = table_ref[band, 0, 0, rows, :]
        base_sin = table_ref[band, 0, 1, rows, :]
        turn_cos = table_ref[band, 1, 0, rows, :]
        turn_sin = table_ref[band, 1, 1, rows, :]
        for q in range(PAD // 128):
            at_cos = turn_cos[:, q:q + 1]
            at_sin = turn_sin[:, q:q + 1]
            lane = slice(q * 128, (q + 1) * 128)
            waves = (
                base_cos * at_cos + base_sin * at_sin,
                base_sin * at_cos - base_cos * at_sin,
            )
            for part in range(2):
                high, low = split(waves[part])
                tabs[c][mine, 0, part, :, lane] = high
                tabs[c][mine, 1, part, :, lane] = low

    raw_copy = pltpu.make_async_copy(x_ref, raw, raw_sem)
    raw_copy.start()
    barrier = pltpu.get_barrier_semaphore()
    pl.semaphore_signal(barrier, inc=1, device_id={"freq": other}, device_id_type=MESH)
    for hop in range(1, wins):
        pl.semaphore_signal(
            barrier, inc=1, device_id={"win": lax.rem(win + hop, wins)}, device_id_type=MESH
        )

    @pl.when(has_right)
    def _():
        pl.semaphore_signal(barrier, inc=1, device_id={"sta": sta + 1}, device_id_type=MESH)

    @pl.when(has_left)
    def _():
        pl.semaphore_signal(barrier, inc=1, device_id={"sta": sta - 1}, device_id_type=MESH)

    edge = SAMPLES // 20
    span = -(-edge // 8) * 8
    begin = pl.multiple_of(freq * (samples - span), 8)
    at = begin + lax.broadcasted_iota(jnp.int32, (span, lanes), 0)
    position = jnp.where(freq == 0, at, samples - 1 - at)
    ramp = 0.5 * (1.0 - jnp.cos(math.pi * (position.astype(jnp.float32) + 0.5) / edge))
    ramp = jnp.where(position < edge, ramp, 1.0)
    raw_copy.wait()
    for w in range(local_wins):
        part = slice(w * lanes, (w + 1) * lanes)
        raw[w, pl.ds(begin, span), :] = raw[w, pl.ds(begin, span), :] * ramp
        high, low = split(raw[w])
        xh[:samples, part] = high
        xl[:samples, part] = low
    blank = jnp.zeros((PAD - samples, cols), jnp.bfloat16)
    xh[samples:] = blank
    xl[samples:] = blank

    for mine in range(2):
        fill(0, mine)

    ends = jnp.where(has_right, 1, 0) + jnp.where(has_left, 1, 0)
    pl.semaphore_wait(barrier, wins + ends)

    def partial(c, mine):
        rows = sizes[c]
        odd = lax.broadcasted_iota(jnp.int32, (2 * rows, 1), 0) % 2
        sign = jnp.where((odd == 0) & (freq == 1), -1.0, 1.0).astype(jnp.float32)
        both = dot(tabs[c][mine].reshape(4 * rows, PAD), xh[...])
        rest = dot(tabs[c][mine, 0].reshape(2 * rows, PAD), xl[...])
        value = (both[:2 * rows] + (both[2 * rows:] + rest)) * sign
        return value.reshape(2, rows, cols)

    def freq_copy(c):
        return pltpu.make_async_remote_copy(
            src_ref=gives[c], dst_ref=gots[c],
            send_sem=fs_sem.at[c], recv_sem=fr_sem.at[c],
            device_id={"freq": other}, device_id_type=MESH,
        )

    def transform(c, between=None):
        rows = pl.ds(pl.multiple_of(starts[c], 16), sizes[c])
        gives[c][...] = partial(c, 0)
        freq_copy(c).start()
        value = partial(c, 1)
        if between is not None:
            between()
        freq_copy(c).wait_recv()
        value = value + gots[c][...]
        spec[:, rows, :] = value
        mag[rows, :] = jnp.sqrt(value[0] * value[0] + value[1] * value[1])

    station = lax.broadcasted_iota(jnp.int32, (1, cols), 1) % lanes
    live = (station < live_ref[0]).astype(jnp.float32)

    def encode(hop, start, count):
        dest = lax.rem(win + hop, wins)
        bin_at = freq * BAND + dest * sub + lax.broadcasted_iota(jnp.int32, (sub, count), 0)
        near = start + freq * (BAND - HALO) + lax.broadcasted_iota(jnp.int32, (sub, count), 1)
        box = (near - bin_at <= HALF_WIDTH) & (bin_at - near <= HALF_WIDTH)
        box = box.astype(jnp.float32).astype(jnp.bfloat16)
        high, low = split(mag[pl.ds(pl.multiple_of(start, 16), count), :])
        summed = dot(box, high) + dot(box, low)
        bin_at = freq * BAND + dest * sub + lax.broadcasted_iota(jnp.int32, (sub, 1), 0)
        counted = (
            jnp.minimum(bin_at + HALF_WIDTH, BINS - 1) - jnp.maximum(bin_at - HALF_WIDTH, 0) + 1
        ).astype(jnp.float32)
        inverse = live / jnp.maximum(summed / counted, AMP_FLOOR)
        rows = pl.ds(pl.multiple_of(freq * HALO + dest * sub, 16), sub)
        real = spec[0, rows, :] * inverse
        imag = spec[1, rows, :] * inverse
        for w in range(local_wins):
            re = real[:, w * lanes:(w + 1) * lanes]
            im = imag[:, w * lanes:(w + 1) * lanes]
            peak = jnp.max(jnp.maximum(jnp.abs(re), jnp.abs(im)), axis=0, keepdims=True)
            level = jnp.ceil(jnp.log2(jnp.maximum(peak, 1e-30)) * 4.0 + 0.01)
            factor = jnp.exp2(level * -0.25) * LEVELS
            top = jnp.round(re * factor).astype(jnp.int32)
            bottom = jnp.round(im * factor).astype(jnp.int32)
            codes[hop, pl.ds(w, sub, stride=local_wins), :] = top * 65536 + (bottom & 65535)
            codes[hop, pl.ds(sub * local_wins + w, 1), :] = level.astype(jnp.int32)

    def win_copy(hop):
        return pltpu.make_async_remote_copy(
            src_ref=codes.at[hop], dst_ref=out_ref.at[sta, win],
            send_sem=ws_sem.at[hop], recv_sem=wr_sem.at[hop],
            device_id={"win": lax.rem(win + hop, wins)}, device_id_type=MESH,
        )

    def slot(block, j):
        return out_ref.at[block, lax.rem(win - j + wins, wins)]

    def right_copy(block, t, j, own=False):
        return pltpu.make_async_remote_copy(
            src_ref=codes.at[0] if own else slot(block, j), dst_ref=slot(block, j),
            send_sem=rs_sem.at[t, j], recv_sem=rr_sem.at[t, j],
            device_id={"sta": sta + 1}, device_id_type=MESH,
        )

    def left_copy(block, t, j, own=False):
        return pltpu.make_async_remote_copy(
            src_ref=codes.at[0] if own else slot(block, j), dst_ref=slot(block, j),
            send_sem=ls_sem.at[t, j], recv_sem=lr_sem.at[t, j],
            device_id={"sta": sta - 1}, device_id_type=MESH,
        )

    def depart(j):
        @pl.when(has_right)
        def _():
            right_copy(sta, 0, j, j == 0).start()

        @pl.when(has_left)
        def _():
            left_copy(sta, 0, j, j == 0).start()

    def relay(low, high, j):
        def step(t, carry):
            @pl.when(sta - t >= 0)
            def _():
                right_copy(sta - t, t - 1, j).wait_recv()

                @pl.when(has_right)
                def _():
                    right_copy(sta - t, t, j).start()

            @pl.when(sta + t < stas)
            def _():
                left_copy(sta + t, t - 1, j).wait_recv()

                @pl.when(has_left)
                def _():
                    left_copy(sta + t, t, j).start()

            return carry

        lax.fori_loop(low, high, step, 0)

    transform(0)
    encode(0, starts[0], sizes[0])
    depart(0)
    for c in range(1, len(sizes)):
        for mine in range(2):
            fill(c, mine)
    keep = pltpu.make_async_copy(codes.at[0], out_ref.at[sta, win], own_sem)
    keep.start()
    early = min(2, stas)
    if len(sizes) == 2:
        transform(1, lambda: relay(1, early, 0))
    for hop in range(1, wins):
        encode(hop, 0, ROWS)
        win_copy(hop).start()
    if len(sizes) == 1:
        relay(1, early, 0)
    late = min(3, stas)
    relay(early, late, 0)
    for j in range(1, wins):
        win_copy(j).wait_recv()
        depart(j)
    relay(late, stas, 0)
    for j in range(1, wins):
        relay(1, stas, j)

    def drain(t, carry):
        for j in range(wins):
            @pl.when(has_right & (sta - t >= 0))
            def _(j=j):
                right_copy(sta - t, t, j).wait_send()

            @pl.when(has_left & (sta + t < stas))
            def _(j=j):
                left_copy(sta + t, t, j).wait_send()
        return carry

    lax.fori_loop(0, stas - 1, drain, 0)
    for c in range(len(sizes)):
        freq_copy(c).wait_send()
    for hop in range(1, wins):
        win_copy(hop).wait_send()
    keep.wait()


def gathered_codes(live, x, table):
    stas = lax.axis_size("sta")
    wins = lax.axis_size("win")
    local_wins, samples, lanes = x.shape
    cols = local_wins * lanes
    rows = BAND // wins * local_wins + 8
    dma = pltpu.SemaphoreType.DMA
    chunks = []
    for size in chunk_rows(wins):
        chunks.append(pltpu.VMEM((2, 2, 2, size, PAD), jnp.bfloat16))
        chunks += [pltpu.VMEM((2, size, cols), jnp.float32)] * 2
    hold = pl.BlockSpec(memory_space=pl.ANY)
    return pl.pallas_call(
        functools.partial(spectra_kernel, stas, wins, local_wins),
        out_shape=jax.ShapeDtypeStruct((stas, wins, rows, lanes), jnp.int32),
        in_specs=[
            pl.BlockSpec(memory_space=pltpu.SMEM), hold, pl.BlockSpec(memory_space=pltpu.VMEM),
        ],
        out_specs=pl.BlockSpec(memory_space=pltpu.VMEM),
        scratch_shapes=[
            pltpu.VMEM((local_wins, samples, lanes), jnp.float32),
            pltpu.VMEM((PAD, cols), jnp.bfloat16),
            pltpu.VMEM((PAD, cols), jnp.bfloat16),
            pltpu.VMEM((2, ROWS, cols), jnp.float32),
            pltpu.VMEM((ROWS, cols), jnp.float32),
            pltpu.VMEM((wins, rows, lanes), jnp.int32),
            dma(()), dma((2,)), dma((2,)), dma((wins,)), dma((wins,)),
            dma((stas, wins)), dma((stas, wins)), dma((stas, wins)), dma((stas, wins)), dma(()),
        ] + chunks,
        compiler_params=pltpu.CompilerParams(
            collective_id=0, has_side_effects=True, vmem_limit_bytes=62 << 20
        ),
        name="spectra",
    )(live, x, table)


def pair_kernel(wins, local_wins, group, steps, slots_ref, left_ref, right_ref, out_ref):
    step = pl.program_id(1)
    lanes = left_ref.shape[-1]
    span = group * local_wins
    half = wins * span
    depth = 2 * half
    scale_row = left_ref.shape[2] - 8
    bins = out_ref.shape[1]
    factor = 1.0 / math.sqrt(wins * local_wins)

    odd = lax.broadcasted_iota(jnp.int32, (span, lanes), 0) % local_wins

    def levels(ref, scale):
        found = []
        for s in range(wins):
            level = jnp.zeros((span, lanes), jnp.float32)
            for w in range(local_wins):
                row = ref[0, s, scale_row + w:scale_row + w + 1, :].astype(jnp.float32)
                level = jnp.where(odd == w, jnp.exp2(row * 0.25) * scale, level)
            found.append(level)
        return found

    left_levels = levels(left_ref, 1.0 / LEVELS)
    right_levels = levels(right_ref, factor / LEVELS)

    def decoded(ref, first, found):
        planes = ([], [])
        for s in range(wins):
            word = ref[0, s, pl.ds(pl.multiple_of(first * local_wins, 8), span), :]
            level = found[s]
            planes[0].append((word >> 16).astype(jnp.float32) * level)
            planes[1].append(((word << 16) >> 16).astype(jnp.float32) * level)
        return jnp.concatenate(planes[0], axis=0), jnp.concatenate(planes[1], axis=0)

    def turned(value):
        high = value.astype(jnp.bfloat16).astype(jnp.float32)
        both = jnp.concatenate([high, value - high], axis=0)
        return both.T.astype(jnp.bfloat16)

    row_bin = lax.broadcasted_iota(jnp.int32, (depth, 2 * lanes), 0) // local_wins % group
    col_odd = lax.broadcasted_iota(jnp.int32, (depth, 2 * lanes), 1) // lanes
    keep = row_bin % 2 == col_odd
    lane_pair = lax.broadcasted_iota(jnp.int32, (lanes, 2 * depth), 1) // local_wins % group // 2

    for g in range(bins // group):
        first = step * bins + g * group
        left_re, left_im = decoded(left_ref, first, left_levels)
        right_re, right_im = decoded(right_ref, first, right_levels)
        streams = (
            turned(jnp.concatenate([left_re, left_im], axis=0)),
            turned(jnp.concatenate([left_im, -left_re], axis=0)),
        )
        held = jnp.concatenate([right_re, right_im], axis=0)
        held = jnp.where(keep, jnp.concatenate([held, held], axis=1), 0.0)
        high, low = split(held)
        held = jnp.concatenate([high, high, low, low], axis=0)
        for m in range(group // 2):
            for p in range(2):
                part = jnp.where(lane_pair == m, streams[p], jnp.zeros_like(streams[p]))
                part = jnp.concatenate([part, part], axis=1)
                out = jnp.dot(part, held, preferred_element_type=jnp.float32)
                out = out.astype(jnp.bfloat16)
                out_ref[0, g * group + 2 * m, p] = out[:, :lanes]
                out_ref[0, g * group + 2 * m + 1, p] = out[:, lanes:]


def pair_products(codes, slots, local_wins):
    stas, wins, rows, lanes = codes.shape
    bins = (rows - 8) // local_wins
    group = max(4, 64 // (2 * wins * local_wins))
    chunk = min(32, bins)
    count = slots.shape[0]
    spec = pltpu.PrefetchScalarGridSpec(
        num_scalar_prefetch=1,
        grid=(count, bins // chunk),
        in_specs=[
            pl.BlockSpec((1, wins, rows, lanes), lambda i, j, s: (s[i, 0], 0, 0, 0)),
            pl.BlockSpec((1, wins, rows, lanes), lambda i, j, s: (s[i, 1], 0, 0, 0)),
        ],
        out_specs=pl.BlockSpec((1, chunk, 2, lanes, lanes), lambda i, j, s: (i, j, 0, 0, 0)),
    )
    return pl.pallas_call(
        functools.partial(pair_kernel, wins, local_wins, group, bins // chunk),
        out_shape=jax.ShapeDtypeStruct((count, bins, 2, lanes, lanes), jnp.bfloat16),
        grid_spec=spec,
        compiler_params=pltpu.CompilerParams(vmem_limit_bytes=62 << 20),
        name="pairs",
    )(slots, codes, codes)


def local(table, records, valid_counts, pair_blocks):
    local_wins = records.shape[1]
    codes = gathered_codes(valid_counts, jnp.transpose(records, (1, 2, 0)), jnp.asarray(table))
    slots = pair_blocks.shape[0] // lax.axis_size("sta")
    mine = lax.dynamic_slice_in_dim(pair_blocks, lax.axis_index("sta") * slots, slots, 0)
    return pair_products(codes, mine, local_wins)[:, None]


def solution(mesh):
    in_specs = (P(("group", "sta"), "win", "freq"), P(("group", "sta")), P("group", None))
    out_specs = P(("group", "sta"), "freq", "win", None, None, None)
    body = functools.partial(local, dft_factors())
    return jax.shard_map(body, mesh=mesh, in_specs=in_specs, out_specs=out_specs, check_vma=False)
```

```python
import functools
import math

import jax
import jax.numpy as jnp
import numpy as np
from jax import lax
from jax.experimental import pallas as pl
from jax.experimental.pallas import tpu as pltpu
from jax.sharding import PartitionSpec as P

SAMPLES = 3600
BINS = 512
HALF_WIDTH = 10
AMP_FLOOR = 0.1
HALO = 16
PAD = 1920
BAND = BINS // 2
ROWS = BAND + HALO
LEVELS = 32766.0
MESH = pl.DeviceIdType.MESH


def band_bins(band):
    own = np.arange(BAND) + band * BAND
    halo = np.arange(HALO) + (BAND if band == 0 else BAND - HALO)
    return np.concatenate([own, halo])


def dft_table():
    half = SAMPLES // 2
    table = np.zeros((2, 2, 2, ROWS, PAD), jnp.bfloat16)
    for band in range(2):
        phase = (band_bins(band)[:, None] + 1) * np.arange(half)[None] % SAMPLES
        angle = phase * (2.0 * math.pi / SAMPLES)
        for part, wave in enumerate((np.cos(angle), -np.sin(angle))):
            value = wave / math.sqrt(SAMPLES)
            high = value.astype(jnp.bfloat16)
            table[band, part, 0, :, :half] = high
            table[band, part, 1, :, :half] = (value - high.astype(np.float64)).astype(jnp.bfloat16)
    return table


def split(value):
    high = value.astype(jnp.bfloat16)
    return high, (value - high.astype(jnp.float32)).astype(jnp.bfloat16)


def dot(a, b):
    return jnp.dot(a, b, preferred_element_type=jnp.float32)


def spectra_kernel(
    stas, wins, local_wins, live_ref, x_ref, table_ref, out_ref,
    tab, raw, xh, xl, give, got, own, codes,
    tab_sem, raw_sem, fs_sem, fr_sem, ws_sem, wr_sem, rs_sem, rr_sem, ls_sem, lr_sem, own_sem,
):
    sta = lax.axis_index("sta")
    win = lax.axis_index("win")
    freq = lax.axis_index("freq")
    other = 1 - freq
    samples, lanes = x_ref.shape[1:]
    sub = BAND // wins
    has_right = sta < stas - 1
    has_left = sta > 0

    def table_copy(step):
        band = other if step < 2 else freq
        return pltpu.make_async_copy(
            table_ref.at[band, step % 2], tab.at[step], tab_sem.at[step]
        )

    raw_copy = pltpu.make_async_copy(x_ref, raw, raw_sem)
    raw_copy.start()
    for step in range(4):
        table_copy(step).start()

    barrier = pltpu.get_barrier_semaphore()
    pl.semaphore_signal(barrier, inc=1, device_id={"freq": other}, device_id_type=MESH)
    for hop in range(1, wins):
        pl.semaphore_signal(
            barrier, inc=1, device_id={"win": lax.rem(win + hop, wins)}, device_id_type=MESH
        )

    @pl.when(has_right)
    def _():
        pl.semaphore_signal(barrier, inc=1, device_id={"sta": sta + 1}, device_id_type=MESH)

    @pl.when(has_left)
    def _():
        pl.semaphore_signal(barrier, inc=1, device_id={"sta": sta - 1}, device_id_type=MESH)

    edge = SAMPLES // 20
    span = -(-edge // 8) * 8
    begin = pl.multiple_of(freq * (samples - span), 8)
    at = begin + lax.broadcasted_iota(jnp.int32, (span, lanes), 0)
    position = jnp.where(freq == 0, at, samples - 1 - at)
    ramp = 0.5 * (1.0 - jnp.cos(math.pi * (position.astype(jnp.float32) + 0.5) / edge))
    ramp = jnp.where(position < edge, ramp, 1.0)
    raw_copy.wait()
    for w in range(local_wins):
        part = slice(w * lanes, (w + 1) * lanes)
        raw[w, pl.ds(begin, span), :] = raw[w, pl.ds(begin, span), :] * ramp
        high, low = split(raw[w])
        xh[:samples, part] = high
        xl[:samples, part] = low
    blank = jnp.zeros((PAD - samples, local_wins * lanes), jnp.bfloat16)
    xh[samples:] = blank
    xl[samples:] = blank

    ends = jnp.where(has_right, 1, 0) + jnp.where(has_left, 1, 0)
    pl.semaphore_wait(barrier, wins + ends)

    odd = lax.broadcasted_iota(jnp.int32, (ROWS, 1), 0) % 2
    sign = jnp.where((odd == 0) & (freq == 1), -1.0, 1.0).astype(jnp.float32)

    def partial(step):
        table_copy(step).wait()
        value = dot(tab[step, 0], xh[...]) + (
            dot(tab[step, 0], xl[...]) + dot(tab[step, 1], xh[...])
        )
        return value * sign

    def freq_copy(step):
        return pltpu.make_async_remote_copy(
            src_ref=give.at[step], dst_ref=got.at[step],
            send_sem=fs_sem.at[step], recv_sem=fr_sem.at[step],
            device_id={"freq": other}, device_id_type=MESH,
        )

    for step in range(2):
        give[step] = partial(step)
        freq_copy(step).start()
    for step in range(2):
        own[step] = partial(2 + step)
    for step in range(2):
        freq_copy(step).wait()

    real = own[0] + got[0]
    imag = own[1] + got[1]
    magnitude = jnp.sqrt(real * real + imag * imag)
    row = lax.broadcasted_iota(jnp.int32, (BAND, ROWS), 0)
    col = lax.broadcasted_iota(jnp.int32, (BAND, ROWS), 1)
    place = jnp.where(col < BAND, col, jnp.where(freq == 0, col, col - BAND - HALO))
    box = ((place - row <= HALF_WIDTH) & (row - place <= HALF_WIDTH)).astype(jnp.float32)
    box = box.astype(jnp.bfloat16)
    mag_high, mag_low = split(magnitude)
    summed = jnp.dot(box, mag_high, preferred_element_type=jnp.float32) + jnp.dot(
        box, mag_low, preferred_element_type=jnp.float32
    )
    bin_at = freq * BAND + lax.broadcasted_iota(jnp.int32, (BAND, 1), 0)
    counted = (
        jnp.minimum(bin_at + HALF_WIDTH, BINS - 1) - jnp.maximum(bin_at - HALF_WIDTH, 0) + 1
    ).astype(jnp.float32)
    station = lax.broadcasted_iota(jnp.int32, (1, local_wins * lanes), 1) % lanes
    live = (station < live_ref[0]).astype(jnp.float32)
    inverse = live / jnp.maximum(summed / counted, AMP_FLOOR)
    real = real[:BAND] * inverse
    imag = imag[:BAND] * inverse

    for dest in range(wins):
        for w in range(local_wins):
            re = real[dest * sub:(dest + 1) * sub, w * lanes:(w + 1) * lanes]
            im = imag[dest * sub:(dest + 1) * sub, w * lanes:(w + 1) * lanes]
            peak = jnp.max(jnp.maximum(jnp.abs(re), jnp.abs(im)), axis=0, keepdims=True)
            level = jnp.ceil(jnp.log2(jnp.maximum(peak, 1e-30)) * 4.0 + 0.01)
            factor = jnp.exp2(level * -0.25) * LEVELS
            top = jnp.round(re * factor).astype(jnp.int32)
            bottom = jnp.round(im * factor).astype(jnp.int32)
            codes[dest, pl.ds(w, sub, stride=local_wins), :] = top * 65536 + (bottom & 65535)
            codes[dest, pl.ds(sub * local_wins + w, 1), :] = level.astype(jnp.int32)

    def win_copy(hop):
        to = lax.rem(win + hop, wins)
        return pltpu.make_async_remote_copy(
            src_ref=codes.at[to], dst_ref=out_ref.at[sta, win],
            send_sem=ws_sem.at[hop], recv_sem=wr_sem.at[hop],
            device_id={"win": to}, device_id_type=MESH,
        )

    for hop in range(1, wins):
        win_copy(hop).start()
    keep = pltpu.make_async_copy(codes.at[win], out_ref.at[sta, win], own_sem)
    keep.start()
    keep.wait()

    def slot(block, j):
        return out_ref.at[block, lax.rem(win - j + wins, wins)]

    def right_copy(block, t, j):
        return pltpu.make_async_remote_copy(
            src_ref=slot(block, j), dst_ref=slot(block, j),
            send_sem=rs_sem.at[t, j], recv_sem=rr_sem.at[t, j],
            device_id={"sta": sta + 1}, device_id_type=MESH,
        )

    def left_copy(block, t, j):
        return pltpu.make_async_remote_copy(
            src_ref=slot(block, j), dst_ref=slot(block, j),
            send_sem=ls_sem.at[t, j], recv_sem=lr_sem.at[t, j],
            device_id={"sta": sta - 1}, device_id_type=MESH,
        )

    for j in range(wins):
        if j > 0:
            win_copy(j).wait_recv()

        @pl.when(has_right)
        def _(j=j):
            right_copy(sta, 0, j).start()

        @pl.when(has_left)
        def _(j=j):
            left_copy(sta, 0, j).start()

    def relay(t, carry):
        for j in range(wins):
            @pl.when(sta - t >= 0)
            def _(j=j):
                right_copy(sta - t, t - 1, j).wait_recv()

                @pl.when(has_right)
                def _():
                    right_copy(sta - t, t, j).start()

            @pl.when(sta + t < stas)
            def _(j=j):
                left_copy(sta + t, t - 1, j).wait_recv()

                @pl.when(has_left)
                def _():
                    left_copy(sta + t, t, j).start()
        return carry

    lax.fori_loop(1, stas, relay, 0)

    def drain(t, carry):
        for j in range(wins):
            @pl.when(has_right & (sta - t >= 0))
            def _(j=j):
                right_copy(sta - t, t, j).wait_send()

            @pl.when(has_left & (sta + t < stas))
            def _(j=j):
                left_copy(sta + t, t, j).wait_send()
        return carry

    lax.fori_loop(0, stas - 1, drain, 0)
    for hop in range(1, wins):
        win_copy(hop).wait_send()


def gathered_codes(live, x, table):
    stas = lax.axis_size("sta")
    wins = lax.axis_size("win")
    local_wins, samples, lanes = x.shape
    cols = local_wins * lanes
    rows = BAND // wins * local_wins + 8
    dma = pltpu.SemaphoreType.DMA
    hold = pl.BlockSpec(memory_space=pl.ANY)
    return pl.pallas_call(
        functools.partial(spectra_kernel, stas, wins, local_wins),
        out_shape=jax.ShapeDtypeStruct((stas, wins, rows, lanes), jnp.int32),
        in_specs=[pl.BlockSpec(memory_space=pltpu.SMEM), hold, hold],
        out_specs=pl.BlockSpec(memory_space=pltpu.VMEM),
        scratch_shapes=[
            pltpu.VMEM((4, 2, ROWS, PAD), jnp.bfloat16),
            pltpu.VMEM((local_wins, samples, lanes), jnp.float32),
            pltpu.VMEM((PAD, cols), jnp.bfloat16),
            pltpu.VMEM((PAD, cols), jnp.bfloat16),
            pltpu.VMEM((2, ROWS, cols), jnp.float32),
            pltpu.VMEM((2, ROWS, cols), jnp.float32),
            pltpu.VMEM((2, ROWS, cols), jnp.float32),
            pltpu.VMEM((wins, rows, lanes), jnp.int32),
            dma((4,)), dma(()), dma((2,)), dma((2,)), dma((wins,)), dma((wins,)),
            dma((stas, wins)), dma((stas, wins)), dma((stas, wins)), dma((stas, wins)), dma(()),
        ],
        compiler_params=pltpu.CompilerParams(
            collective_id=0, has_side_effects=True, vmem_limit_bytes=48 << 20
        ),
        name="spectra",
    )(live, x, table)


def pair_kernel(wins, local_wins, group, steps, slots_ref, left_ref, right_ref, out_ref):
    step = pl.program_id(1)
    lanes = left_ref.shape[-1]
    span = group * local_wins
    half = wins * span
    depth = 2 * half
    scale_row = left_ref.shape[2] - 8
    bins = out_ref.shape[1]
    factor = 1.0 / math.sqrt(wins * local_wins)

    odd = lax.broadcasted_iota(jnp.int32, (span, lanes), 0) % local_wins

    def levels(ref, scale):
        found = []
        for s in range(wins):
            level = jnp.zeros((span, lanes), jnp.float32)
            for w in range(local_wins):
                row = ref[0, s, scale_row + w:scale_row + w + 1, :].astype(jnp.float32)
                level = jnp.where(odd == w, jnp.exp2(row * 0.25) * scale, level)
            found.append(level)
        return found

    left_levels = levels(left_ref, 1.0 / LEVELS)
    right_levels = levels(right_ref, factor / LEVELS)

    def decoded(ref, first, found):
        planes = ([], [])
        for s in range(wins):
            word = ref[0, s, pl.ds(pl.multiple_of(first * local_wins, 8), span), :]
            level = found[s]
            planes[0].append((word >> 16).astype(jnp.float32) * level)
            planes[1].append(((word << 16) >> 16).astype(jnp.float32) * level)
        return jnp.concatenate(planes[0], axis=0), jnp.concatenate(planes[1], axis=0)

    def turned(value):
        high = value.astype(jnp.bfloat16).astype(jnp.float32)
        both = jnp.concatenate([high, value - high], axis=0)
        return both.T.astype(jnp.bfloat16)

    row_bin = lax.broadcasted_iota(jnp.int32, (depth, 2 * lanes), 0) // local_wins % group
    col_odd = lax.broadcasted_iota(jnp.int32, (depth, 2 * lanes), 1) // lanes
    keep = row_bin % 2 == col_odd
    lane_pair = lax.broadcasted_iota(jnp.int32, (lanes, 2 * depth), 1) // local_wins % group // 2

    for g in range(bins // group):
        first = step * bins + g * group
        left_re, left_im = decoded(left_ref, first, left_levels)
        right_re, right_im = decoded(right_ref, first, right_levels)
        streams = (
            turned(jnp.concatenate([left_re, left_im], axis=0)),
            turned(jnp.concatenate([left_im, -left_re], axis=0)),
        )
        held = jnp.concatenate([right_re, right_im], axis=0)
        held = jnp.where(keep, jnp.concatenate([held, held], axis=1), 0.0)
        high, low = split(held)
        held = jnp.concatenate([high, high, low, low], axis=0)
        for m in range(group // 2):
            for p in range(2):
                part = jnp.where(lane_pair == m, streams[p], jnp.zeros_like(streams[p]))
                part = jnp.concatenate([part, part], axis=1)
                out = jnp.dot(part, held, preferred_element_type=jnp.float32)
                out = out.astype(jnp.bfloat16)
                out_ref[0, g * group + 2 * m, p] = out[:, :lanes]
                out_ref[0, g * group + 2 * m + 1, p] = out[:, lanes:]


def pair_products(codes, slots, local_wins):
    stas, wins, rows, lanes = codes.shape
    bins = (rows - 8) // local_wins
    group = max(4, 64 // (2 * wins * local_wins))
    chunk = min(32, bins)
    count = slots.shape[0]
    spec = pltpu.PrefetchScalarGridSpec(
        num_scalar_prefetch=1,
        grid=(count, bins // chunk),
        in_specs=[
            pl.BlockSpec((1, wins, rows, lanes), lambda i, j, s: (s[i, 0], 0, 0, 0)),
            pl.BlockSpec((1, wins, rows, lanes), lambda i, j, s: (s[i, 1], 0, 0, 0)),
        ],
        out_specs=pl.BlockSpec((1, chunk, 2, lanes, lanes), lambda i, j, s: (i, j, 0, 0, 0)),
    )
    return pl.pallas_call(
        functools.partial(pair_kernel, wins, local_wins, group, bins // chunk),
        out_shape=jax.ShapeDtypeStruct((count, bins, 2, lanes, lanes), jnp.bfloat16),
        grid_spec=spec,
        compiler_params=pltpu.CompilerParams(vmem_limit_bytes=32 << 20),
        name="pairs",
    )(slots, codes, codes)


def local(table, records, valid_counts, pair_blocks):
    local_wins = records.shape[1]
    codes = gathered_codes(valid_counts, jnp.transpose(records, (1, 2, 0)), jnp.asarray(table))
    slots = pair_blocks.shape[0] // lax.axis_size("sta")
    mine = lax.dynamic_slice_in_dim(pair_blocks, lax.axis_index("sta") * slots, slots, 0)
    return pair_products(codes, mine, local_wins)[:, None]


def solution(mesh):
    in_specs = (P(("group", "sta"), "win", "freq"), P(("group", "sta")), P("group", None))
    out_specs = P(("group", "sta"), "freq", "win", None, None, None)
    body = functools.partial(local, dft_table())
    return jax.shard_map(body, mesh=mesh, in_specs=in_specs, out_specs=out_specs, check_vma=False)
```
